256 devices in a mesh: ctx: 32 (over y, x, core), tp: 8 (over z).
Axes of the slice: x: 4, y: 4, z: 8, core: 2. Of those that a mesh axis runs over, the one named last changes fastest.
Arguments:
- query_rows: bfloat16 [32768, 4096], P('ctx', 'tp'), may hold values from -6 to 6
- key_rows: bfloat16 [32768, 4096], P('ctx', 'tp'), may hold values from -6 to 6
- value_rows: bfloat16 [32768, 4096], P('ctx', 'tp'), may hold values from -6 to 6
- layer_grad: bfloat16 [32768, 4096], P('ctx', 'tp'), may hold values from -6 to 6
- out_weight: bfloat16 [4096, 4096], P('tp'), may hold values from -0.09375 to 0.09375
Outputs:
- query_grad: bfloat16 [32768, 4096], P('ctx', 'tp')
- key_grad: bfloat16 [32768, 4096], P('ctx', 'tp')
- value_grad: bfloat16 [32768, 4096], P('ctx', 'tp')
The draws below stay inside these ranges and needn't reach their ends.
All inputs are finite; a program needn't handle non-finite values.
Results may differ from the reference program's by a relative error of at most 0.0058.
Values may be sent and summed in bfloat16 or wider, within the bound.
No kernel may reach another device: no remote copies, remote signals or barrier semaphores. Data moves between devices by JAX's collectives and lax.ppermute only.
A program may use at most 128 MiB of HBM per device.

```python
import jax
import jax.numpy as jnp
from jax import lax

D = 4096
HEADS = 32
HEAD = 128
TOK_DEV = 1024
TOKENS = 32768
N_CTX = 32


def level_of(key, extent, split, smallest, top_value):
    def one(dim, blocks):
        heights = jax.random.uniform(jax.random.fold_in(jax.random.fold_in(key, 6), dim), (blocks,), jnp.float32, smallest / len(split), top_value / len(split))
        return jnp.repeat(jnp.exp(heights), extent[dim] // blocks).reshape((-1,) + (1,) * (len(extent) - dim - 1))

    gain = one(*split[0])
    for cut in split[1:]:
        gain = gain * one(*cut)
    return gain


def noise(stream_key, shape, spread, most, cuts=(), kind=jnp.bfloat16):
    gain = level_of(stream_key, shape, cuts, -0.22, 0.18) if cuts else 1.0
    result = jax.random.normal(stream_key, shape, jnp.float32) * spread * gain
    return jnp.minimum(jnp.maximum(result, -most), most).astype(kind)


def setup_inputs(seed: int = 0) -> dict:
    splits = jax.random.split(jax.random.key(seed), 6)
    query_rows = noise(splits[0], (TOKENS, HEADS * HEAD), 1.0, 6.0, ((0, 32), (1, 8)))
    key_rows = noise(splits[1], (TOKENS, HEADS * HEAD), 1.0, 6.0, ((0, 32), (1, 8)))
    value_rows = noise(splits[2], (TOKENS, HEADS * HEAD), 1.0, 6.0, ((0, 32), (1, 8)))
    layer_grad = noise(splits[3], (TOKENS, D), 1.0, 6.0, ((0, 32), (1, 8)))
    out_weight = noise(splits[4], (HEADS * HEAD, D), D ** -0.5, 0.09375, ((0, 8),))
    return dict(query_rows=query_rows, key_rows=key_rows, value_rows=value_rows, layer_grad=layer_grad, out_weight=out_weight)


def block_grads(pieces):
    query_blk, key_blk, value_blk, gradient_block, key_value_state, gradient_state = pieces
    factor = (HEAD * TOKENS) ** -0.5
    positions = jnp.arange(TOK_DEV)
    causal = positions[:, None] >= positions[None, :]
    query_float = query_blk.astype(jnp.float32)
    key_float = key_blk.astype(jnp.float32)
    value_float = value_blk.astype(jnp.float32)
    gradient_float = gradient_block.astype(jnp.float32)
    inside_gradient = jnp.einsum("thv,shv->hts", gradient_float, value_float)
    inside_gradient = jnp.where(causal[None], inside_gradient, jnp.float32(0.0)).astype(jnp.bfloat16).astype(jnp.float32)
    inside_query = jnp.einsum("thk,shk->hts", query_float, key_float)
    inside_query = jnp.where(causal[None], inside_query, jnp.float32(0.0)).astype(jnp.bfloat16).astype(jnp.float32)
    key_value_float = key_value_state.astype(jnp.float32)
    gradient_state_float = gradient_state.astype(jnp.float32)
    query_result = jnp.einsum("vmr,rve->mve", inside_gradient, key_float) + jnp.einsum("nde,dze->ndz", gradient_float, key_value_float)
    key_result = jnp.einsum("cxd,xcr->dcr", inside_gradient, query_float) + jnp.einsum("yqr,qmr->yqm", value_float, gradient_state_float)
    value_result = jnp.einsum("kzx,zkm->xkm", inside_query, gradient_float) + jnp.einsum("jaq,aqd->jad", key_float, gradient_state_float)
    return ((factor * query_result).astype(jnp.bfloat16), (factor * key_result).astype(jnp.bfloat16), (factor * value_result).astype(jnp.bfloat16))


def reference(query_rows, key_rows, value_rows, layer_grad, out_weight):
    grad_heads = jnp.dot(layer_grad, out_weight.T, preferred_element_type=jnp.float32).astype(jnp.bfloat16)
    shape4 = (N_CTX, TOK_DEV, HEADS, HEAD)
    query4 = query_rows.reshape(shape4)
    key4 = key_rows.reshape(shape4)
    value4 = value_rows.reshape(shape4)
    grad4 = grad_heads.reshape(shape4)
    key_value_here = jnp.einsum("cthk,cthv->chkv", key4.astype(jnp.float32), value4.astype(jnp.float32))
    gradient_here = jnp.einsum("cthk,cthv->chkv", query4.astype(jnp.float32), grad4.astype(jnp.float32))
    zero_state = jnp.zeros((1, HEADS, HEAD, HEAD), jnp.float32)
    kv_before = jnp.concatenate([zero_state, jnp.cumsum(key_value_here, 0)[:-1]], 0).astype(jnp.bfloat16)
    reversed_sum = jnp.cumsum(gradient_here[::-1], 0)[::-1]
    grad_after = jnp.concatenate([reversed_sum[1:], zero_state], 0).astype(jnp.bfloat16)
    query_result, key_result, value_result = lax.map(block_grads, (query4, key4, value4, grad4, kv_before, grad_after))
    flat = (TOKENS, HEADS * HEAD)
    return (query_result.reshape(flat), key_result.reshape(flat), value_result.reshape(flat))
```

```python
import functools

import jax
import jax.numpy as jnp
from jax import lax
from jax.experimental import pallas as pl
from jax.experimental.pallas import tpu as pltpu
from jax.sharding import Mesh
from jax.sharding import PartitionSpec as P

HEAD = 128
CHUNK = 256
CTX = ("y", "x", "core")
F32 = jnp.float32
BF16 = jnp.bfloat16
VMEM_BYTES = 16 * 1024 * 1024


def shifted(value, axis, by):
    size = lax.axis_size(axis)
    return lax.ppermute(value, axis, [(i, (i + by) % size) for i in range(size)])


def nt(a, b):
    return lax.dot_general(a, b, (((1,), (1,)), ((), ())), preferred_element_type=F32)


def nn(a, b):
    return lax.dot_general(a, b, (((1,), (0,)), ((), ())), preferred_element_type=F32)


def tn(a, b):
    return lax.dot_general(a, b, (((0,), (0,)), ((), ())), preferred_element_type=F32)


def upper():
    rows = lax.broadcasted_iota(jnp.int32, (CHUNK, CHUNK), 0)
    cols = lax.broadcasted_iota(jnp.int32, (CHUNK, CHUNK), 1)
    return rows <= cols


def before_kernel(q_ref, k_ref, v_ref, inner_ref, parts_ref, total_ref):
    total = None
    keep = upper()
    for i in range(q_ref.shape[0] // CHUNK):
        rows = pl.ds(i * CHUNK, CHUNK)
        k = k_ref[rows, :]
        inner_ref[0, i] = jnp.where(keep, nt(k, q_ref[rows, :]), 0.0).astype(BF16)
        part = tn(k, v_ref[rows, :])
        parts_ref[0, i] = part
        total = part if total is None else total + part
    total_ref[0] = total


def before(q, k, v, heads):
    tokens = q.shape[0]
    chunks = tokens // CHUNK
    head = pl.BlockSpec((tokens, HEAD), lambda h: (0, h))
    return pl.pallas_call(
        before_kernel,
        grid=(heads,),
        in_specs=[head, head, head],
        out_specs=[
            pl.BlockSpec((1, chunks, CHUNK, CHUNK), lambda h: (h, 0, 0, 0)),
            pl.BlockSpec((1, chunks, HEAD, HEAD), lambda h: (h, 0, 0, 0)),
            pl.BlockSpec((1, HEAD, HEAD), lambda h: (h, 0, 0)),
        ],
        out_shape=[
            jax.ShapeDtypeStruct((heads, chunks, CHUNK, CHUNK), BF16),
            jax.ShapeDtypeStruct((heads, chunks, HEAD, HEAD), F32),
            jax.ShapeDtypeStruct((heads, HEAD, HEAD), F32),
        ],
        compiler_params=pltpu.CompilerParams(vmem_limit_bytes=VMEM_BYTES),
        cost_estimate=pl.CostEstimate(
            flops=heads * tokens * (CHUNK + HEAD) * HEAD * 4,
            bytes_accessed=6 * q.size + 2 * heads * tokens * CHUNK,
            transcendentals=0,
        ),
        name="before",
    )(q, k, v)


def grads_kernel(heads, acc_ref, x_ref, w_ref, q_ref, g_ref, parts_ref, total_ref):
    g = (acc_ref[...] + nt(x_ref[...], w_ref[...])).astype(BF16)
    g_ref[...] = g
    first = pl.program_id(0) == 0
    for h in range(heads):
        cols = slice(h * HEAD, (h + 1) * HEAD)
        part = tn(q_ref[:, cols], g[:, cols])
        parts_ref[0, h] = part

        @pl.when(first)
        def _():
            total_ref[h] = part

        @pl.when(jnp.logical_not(first))
        def _():
            total_ref[h] += part


def grads(acc, x, w, q, half, heads):
    tokens, columns = acc.shape
    chunks = tokens // CHUNK
    block = pl.BlockSpec((CHUNK, columns), lambda i: (i, 0))
    return pl.pallas_call(
        functools.partial(grads_kernel, heads),
        grid=(chunks,),
        in_specs=[
            block,
            pl.BlockSpec((CHUNK, x.shape[1]), lambda i: (i, 0)),
            pl.BlockSpec(w.shape, lambda i: (0, 0)),
            pl.BlockSpec((CHUNK, columns), lambda i: (i + half * chunks, 0)),
        ],
        out_specs=[
            block,
            pl.BlockSpec((1, heads, HEAD, HEAD), lambda i: (i, 0, 0, 0)),
            pl.BlockSpec((heads, HEAD, HEAD), lambda i: (0, 0, 0)),
        ],
        out_shape=[
            jax.ShapeDtypeStruct((tokens, columns), BF16),
            jax.ShapeDtypeStruct((chunks, heads, HEAD, HEAD), F32),
            jax.ShapeDtypeStruct((heads, HEAD, HEAD), F32),
        ],
        compiler_params=pltpu.CompilerParams(vmem_limit_bytes=VMEM_BYTES),
        cost_estimate=pl.CostEstimate(
            flops=2 * tokens * columns * (x.shape[1] + HEAD),
            bytes_accessed=6 * acc.size + 4 * x.size + 2 * w.size,
            transcendentals=0,
        ),
        name="grads",
    )(acc, x, w, q)


def inside_kernel(factor, *refs):
    q_ref, k_ref, v_ref, lo_ref, hi_ref, inner_ref, parts_ref, state_ref = refs[:8]
    qg_ref, kg_ref, vg_ref = refs[-3:]
    keep = upper()
    state = state_ref[0].astype(F32)
    chunks = q_ref.shape[0] // CHUNK
    for i in range(chunks):
        rows = pl.ds(i * CHUNK, CHUNK)
        near = lo_ref if i < chunks // 2 else hi_ref
        g = near[pl.ds(i % (chunks // 2) * CHUNK, CHUNK), :]
        q, k, v = q_ref[rows, :], k_ref[rows, :], v_ref[rows, :]
        down = jnp.where(keep, nt(v, g), 0.0).astype(BF16)
        qg = tn(down, k) + nt(g, state.astype(BF16))
        qg_ref[rows, :] = (factor * qg).astype(BF16)
        kg_ref[rows, :] = nn(down, q)
        vg_ref[rows, :] = nn(inner_ref[0, i], g)
        state = state + parts_ref[0, i]


def inside(begin, count, factor, q, k, v, g_lo, g_hi, inner, parts, state, so_far):
    tokens = q.shape[0]
    chunks = tokens // CHUNK
    head = pl.BlockSpec((tokens, HEAD), lambda h: (0, h + begin))
    half = pl.BlockSpec((tokens // 2, HEAD), lambda h: (0, h + begin))
    whole = pl.BlockSpec(memory_space=pl.ANY)
    return pl.pallas_call(
        functools.partial(inside_kernel, factor),
        grid=(count,),
        in_specs=[
            head, head, head, half, half,
            pl.BlockSpec((1, chunks, CHUNK, CHUNK), lambda h: (h + begin, 0, 0, 0)),
            pl.BlockSpec((1, chunks, HEAD, HEAD), lambda h: (h + begin, 0, 0, 0)),
            pl.BlockSpec((1, HEAD, HEAD), lambda h: (h + begin, 0, 0)),
        ] + [whole] * len(so_far),
        out_specs=[head, head, head],
        out_shape=[
            jax.ShapeDtypeStruct(q.shape, BF16),
            jax.ShapeDtypeStruct(q.shape, F32),
            jax.ShapeDtypeStruct(q.shape, F32),
        ],
        input_output_aliases={8 + i: i for i in range(len(so_far))},
        compiler_params=pltpu.CompilerParams(vmem_limit_bytes=VMEM_BYTES),
        cost_estimate=pl.CostEstimate(
            flops=count * tokens * HEAD * (4 * CHUNK + HEAD) * 2,
            bytes_accessed=count * tokens * HEAD * 18,
            transcendentals=0,
        ),
        name=f"inside_{begin}",
    )(q, k, v, g_lo, g_hi, inner, parts, state, *so_far)


def outside_kernel(factor, heads, kg_ref, vg_ref, k_ref, v_ref, lo_ref, hi_ref, state_ref, key_ref, value_ref, after_ref):
    step = pl.program_id(0)
    half = pl.num_programs(0) // 2
    for h in range(heads):
        cols = slice(h * HEAD, (h + 1) * HEAD)

        @pl.when(step == 0)
        def _():
            after_ref[h] = state_ref[h].astype(F32)

        state = after_ref[h].astype(BF16)
        key_ref[:, cols] = (factor * (kg_ref[:, cols] + nt(v_ref[:, cols], state))).astype(BF16)
        value_ref[:, cols] = (factor * (vg_ref[:, cols] + nn(k_ref[:, cols], state))).astype(BF16)

        @pl.when(step < half)
        def _():
            after_ref[h] += hi_ref[0, h]

        @pl.when(step >= half)
        def _():
            after_ref[h] += lo_ref[0, h]


def outside(factor, kg, vg, k, v, parts_lo, parts_hi, state, heads):
    tokens, columns = kg.shape
    chunks = tokens // CHUNK
    half = chunks // 2
    block = pl.BlockSpec((CHUNK, columns), lambda i: (chunks - 1 - i, 0))
    part = (1, heads, HEAD, HEAD)
    return pl.pallas_call(
        functools.partial(outside_kernel, factor, heads),
        grid=(chunks,),
        in_specs=[
            block, block, block, block,
            pl.BlockSpec(part, lambda i: (jnp.minimum(chunks - 1 - i, half - 1), 0, 0, 0)),
            pl.BlockSpec(part, lambda i: (jnp.maximum(half - 1 - i, 0), 0, 0, 0)),
            pl.BlockSpec(state.shape, lambda i: (0, 0, 0)),
        ],
        out_specs=[block, block],
        out_shape=[jax.ShapeDtypeStruct(kg.shape, BF16)] * 2,
        scratch_shapes=[pltpu.VMEM((heads, HEAD, HEAD), F32)],
        compiler_params=pltpu.CompilerParams(vmem_limit_bytes=VMEM_BYTES),
        cost_estimate=pl.CostEstimate(
            flops=4 * tokens * columns * HEAD, bytes_accessed=16 * kg.size, transcendentals=0
        ),
        name="outside",
    )(kg, vg, k, v, parts_lo, parts_hi, state)


def summed(state, later):
    here = {axis: lax.axis_index(axis) for axis in CTX}
    core = here["core"]
    half = state.shape[0] // 2
    mine = lax.dynamic_slice_in_dim(state, half * core, half, 0)
    theirs = lax.dynamic_slice_in_dim(state, half * (1 - core), half, 0)
    partner = shifted(theirs.astype(BF16), "core", 1).astype(F32)
    running = mine + partner
    outer = None
    for axis in ("x", "y"):
        size = lax.axis_size(axis)
        sent = running.astype(BF16)
        for by in range(1, size):
            got = shifted(sent, axis, by).astype(F32)
            source = (here[axis] - by) % size
            counts = source > here[axis] if later else source < here[axis]
            term = jnp.where(counts, got, 0.0)
            outer = term if outer is None else outer + term
            running = running + got
    inner = core == (0 if later else 1)
    for_me = outer + jnp.where(inner, partner, 0.0)
    for_them = outer + jnp.where(inner, 0.0, mine)
    for_me = for_me.astype(BF16)
    received = shifted(for_them.astype(BF16), "core", 1)
    first = core == 0
    return jnp.concatenate(
        [jnp.where(first, for_me, received), jnp.where(first, received, for_me)], 0
    )


def local(query_rows, key_rows, value_rows, layer_grad, out_weight):
    tokens, columns = query_rows.shape
    heads = columns // HEAD
    factor = float((HEAD * tokens * lax.axis_size(CTX)) ** (-0.5))
    ring = lax.axis_size("tp")
    me = lax.axis_index("tp")
    half = tokens // 2

    def weights(source):
        return lax.dynamic_slice_in_dim(out_weight, source % ring * columns, columns, 1)

    right = [layer_grad[:half], layer_grad[half:]]
    left = list(right)
    own = weights(me)
    totals = [nt(part, own) for part in right]
    for hop in range(1, ring // 2):
        right = [shifted(part, "tp", 1) for part in right]
        left = [shifted(part, "tp", -1) for part in left[::-1]][::-1]
        from_right, from_left = weights(me - hop), weights(me + hop)
        totals = [
            total + nt(a, from_right) + nt(b, from_left)
            for total, a, b in zip(totals, right, left)
        ]
    last = [shifted(right[0], "tp", 1), shifted(left[1], "tp", -1)]

    inner, kv_parts, kv_total = before(query_rows, key_rows, value_rows, heads)
    kv_state = summed(kv_total, False)

    far = weights(me + ring // 2)
    g_lo, parts_lo, sum_lo = grads(totals[0], last[0], far, query_rows, 0, heads)
    g_hi, parts_hi, sum_hi = grads(totals[1], last[1], far, query_rows, 1, heads)
    after = summed(sum_lo + sum_hi, True)

    so_far = ()
    for begin in range(heads):
        so_far = inside(
            begin, 1, factor, query_rows, key_rows, value_rows, g_lo, g_hi, inner, kv_parts, kv_state, so_far
        )
    query_grad, kg, vg = so_far
    key_grad, value_grad = outside(
        factor, kg, vg, key_rows, value_rows, parts_lo, parts_hi, after, heads
    )
    return query_grad, key_grad, value_grad


def solution(mesh):
    finer = Mesh(mesh.devices.reshape(4, 4, 2, mesh.shape["tp"]), (*CTX, "tp"))
    return jax.shard_map(
        local,
        mesh=finer,
        in_specs=(P(CTX, "tp"), P(CTX, "tp"), P(CTX, "tp"), P(CTX, "tp"), P("tp", None)),
        out_specs=(P(CTX, "tp"), P(CTX, "tp"), P(CTX, "tp")),
        check_vma=False,
    )
```

```python
import functools

import jax
import jax.numpy as jnp
from jax import lax
from jax.experimental import pallas as pl
from jax.experimental.pallas import tpu as pltpu
from jax.sharding import Mesh
from jax.sharding import PartitionSpec as P


HEAD = 128
CHUNK = 256
CTX = ("y", "x", "core")
F32 = jnp.float32
BF16 = jnp.bfloat16
VMEM_BYTES = 16 * 1024 * 1024
SMALL_BYTES = 4 * 1024 * 1024
VMEM_SPEC = pl.BlockSpec(memory_space=pltpu.VMEM)


def moved(value, axis, by):
    size = lax.axis_size(axis)
    return lax.ppermute(value, axis, [(i, (i + by) % size) for i in range(size)])


def nt(a, b):
    return lax.dot_general(a, b, (((1,), (1,)), ((), ())), preferred_element_type=F32)


def nn(a, b):
    return lax.dot_general(a, b, (((1,), (0,)), ((), ())), preferred_element_type=F32)


def tn(a, b):
    return lax.dot_general(a, b, (((0,), (0,)), ((), ())), preferred_element_type=F32)


def upper():
    rows = lax.broadcasted_iota(jnp.int32, (CHUNK, CHUNK), 0)
    cols = lax.broadcasted_iota(jnp.int32, (CHUNK, CHUNK), 1)
    return rows <= cols


def call(kernel, ins, outs, flops=0, scratch=(), limit=VMEM_BYTES, in_specs=None, out_specs=None):
    shapes = [jax.ShapeDtypeStruct(*out) for out in outs]
    moved_bytes = sum(a.size * a.dtype.itemsize for a in (*ins, *shapes))
    return pl.pallas_call(
        kernel,
        in_specs=in_specs or [VMEM_SPEC] * len(ins),
        out_specs=out_specs or [VMEM_SPEC] * len(outs),
        out_shape=shapes,
        scratch_shapes=scratch,
        compiler_params=pltpu.CompilerParams(vmem_limit_bytes=limit),
        cost_estimate=pl.CostEstimate(flops=flops, bytes_accessed=moved_bytes, transcendentals=0),
    )(*ins)


def before_kernel(heads, q_ref, k_ref, v_ref, inner_ref, parts_ref, mine_ref, theirs_ref, total_ref):
    keep = upper()
    for h in range(heads):
        cols = slice(h * HEAD, (h + 1) * HEAD)
        total = None
        for i in range(q_ref.shape[0] // CHUNK):
            rows = pl.ds(i * CHUNK, CHUNK)
            k = k_ref[rows, cols]
            inner_ref[h, i] = jnp.where(keep, nt(k, q_ref[rows, cols]), 0.0).astype(BF16)
            part = tn(k, v_ref[rows, cols])
            parts_ref[h, i] = part
            total = part if total is None else total + part
        total_ref[h] = total
    share(total_ref, mine_ref, theirs_ref)


def before(q, k, v, heads, wire):
    tokens = q.shape[0]
    chunks = tokens // CHUNK
    half = (heads // 2, HEAD, HEAD)
    return call(
        functools.partial(before_kernel, heads),
        (q, k, v),
        (
            ((heads, chunks, CHUNK, CHUNK), BF16),
            ((heads, chunks, HEAD, HEAD), F32),
            (half, F32),
            (half, wire),
        ),
        flops=heads * tokens * (CHUNK + HEAD) * HEAD * 2,
        scratch=[pltpu.VMEM((heads, HEAD, HEAD), F32)],
    )


PIECES = 4


def split_kernel(x_ref, lo_ref, hi_ref, sems):
    step = lo_ref.shape[0] // PIECES
    copies = []
    for half, ref in enumerate((lo_ref, hi_ref)):
        for i in range(PIECES):
            src = x_ref.at[pl.ds(half * lo_ref.shape[0] + i * step, step), :]
            copies.append(
                pltpu.make_async_copy(src, ref.at[pl.ds(i * step, step), :], sems.at[len(copies)])
            )
            copies[-1].start()
    for copy in copies:
        copy.wait()


def split(x):
    half = ((x.shape[0] // 2, x.shape[1]), x.dtype)
    return call(
        split_kernel,
        (pltpu.with_memory_space_constraint(x, pltpu.HBM),),
        (half, half),
        scratch=[pltpu.SemaphoreType.DMA((2 * PIECES,))],
        limit=SMALL_BYTES,
        in_specs=[pl.BlockSpec(memory_space=pltpu.HBM)],
    )


def weight_of(w_ref, by):
    size = lax.axis_size("tp")
    width = w_ref.shape[1] // size
    source = lax.rem(lax.axis_index("tp") + by + size, size)
    return w_ref[:, pl.ds(pl.multiple_of(source * width, width), width)]


def product_kernel(offsets, w_ref, *refs):
    out_ref = refs[-1]
    total = refs[len(offsets)][...] if len(refs) > len(offsets) + 1 else None
    for by, ref in zip(offsets, refs):
        term = nt(ref[...], weight_of(w_ref, by))
        total = term if total is None else total + term
    out_ref[...] = total


def product(w, parts, offsets, total):
    rows, width = parts[0].shape
    ins = (w, *parts) if total is None else (w, *parts, total)
    (out,) = call(
        functools.partial(product_kernel, offsets),
        ins,
        (((rows, w.shape[0]), F32),),
        flops=2 * rows * width * w.shape[0] * len(parts),
    )
    return out


def share(total_ref, mine_ref, theirs_ref):
    core = lax.axis_index("core")
    half = mine_ref.shape[0]
    for i in range(half):
        mine_ref[i] = total_ref[core * half + i]
        theirs_ref[i] = total_ref[(1 - core) * half + i].astype(theirs_ref.dtype)


def grads_kernel(heads, acc_lo, acc_hi, x_lo, x_hi, w_ref, q_ref, g_ref, parts_ref, mine_ref, theirs_ref, total_ref):
    tokens = q_ref.shape[0]
    chunks = tokens // CHUNK
    far = weight_of(w_ref, lax.axis_size("tp") // 2)
    totals = [None] * heads
    for i in range(chunks):
        acc_ref, x_ref = (acc_lo, x_lo) if i < chunks // 2 else (acc_hi, x_hi)
        near = pl.ds(i % (chunks // 2) * CHUNK, CHUNK)
        rows = pl.ds(i * CHUNK, CHUNK)
        g = (acc_ref[near, :] + nt(x_ref[near, :], far)).astype(BF16)
        g_ref[rows, :] = g
        for h in range(heads):
            cols = slice(h * HEAD, (h + 1) * HEAD)
            part = tn(q_ref[rows, cols], g[:, cols])
            parts_ref[h, i] = part
            totals[h] = part if i == 0 else totals[h] + part
    for h in range(heads):
        total_ref[h] = totals[h]
    share(total_ref, mine_ref, theirs_ref)


def grads(totals, last, w, q, heads, wire):
    tokens, columns = q.shape
    half = (heads // 2, HEAD, HEAD)
    return call(
        functools.partial(grads_kernel, heads),
        (*totals, *last, w, q),
        (
            ((tokens, columns), BF16),
            ((heads, tokens // CHUNK, HEAD, HEAD), F32),
            (half, F32),
            (half, wire),
        ),
        flops=2 * tokens * columns * (columns + HEAD),
        scratch=[pltpu.VMEM((heads, HEAD, HEAD), F32)],
    )


def pair_kernel(mine_ref, partner_ref, sent_ref):
    sent_ref[...] = (mine_ref[...] + partner_ref[...].astype(F32)).astype(sent_ref.dtype)


def counted(axis, later, refs):
    here, size = lax.axis_index(axis), lax.axis_size(axis)
    outer = total = None
    for by, ref in enumerate(refs, 1):
        got = ref[...].astype(F32)
        source = lax.rem(here - by + size, size)
        keep = source > here if later else source < here
        term = jnp.where(keep, got, 0.0)
        outer = term if outer is None else outer + term
        total = got if total is None else total + got
    return outer, total


def row_kernel(axis, later, mine_ref, partner_ref, *refs):
    outer_ref, sent_ref = refs[-2:]
    outer, total = counted(axis, later, refs[:-2])
    outer_ref[...] = outer
    sent_ref[...] = (total + mine_ref[...] + partner_ref[...].astype(F32)).astype(sent_ref.dtype)


def last_kernel(axis, later, mine_ref, partner_ref, outer_ref, *refs):
    me_ref, them_ref = refs[-2:]
    outer, _ = counted(axis, later, refs[:-2])
    outer = outer + outer_ref[...]
    inner = lax.axis_index("core") == (0 if later else 1)
    me_ref[...] = (outer + jnp.where(inner, partner_ref[...].astype(F32), 0.0)).astype(BF16)
    them_ref[...] = (outer + jnp.where(inner, 0.0, mine_ref[...])).astype(BF16)


def summed(mine, theirs, later):
    shape, wire = mine.shape, theirs.dtype
    partner = moved(theirs, "core", 1)
    (sent,) = call(pair_kernel, (mine, partner), ((shape, wire),), limit=SMALL_BYTES)
    got = [moved(sent, "x", by) for by in range(1, lax.axis_size("x"))]
    outer, sent = call(
        functools.partial(row_kernel, "x", later),
        (mine, partner, *got),
        ((shape, F32), (shape, wire)),
        limit=SMALL_BYTES,
    )
    got = [moved(sent, "y", by) for by in range(1, lax.axis_size("y"))]
    for_me, for_them = call(
        functools.partial(last_kernel, "y", later),
        (mine, partner, outer, *got),
        ((shape, BF16), (shape, BF16)),
        limit=SMALL_BYTES,
    )
    return for_me, moved(for_them, "core", 1)


def state_of(h, mine_ref, other_ref):
    half = mine_ref.shape[0]
    mine = lax.axis_index("core") == h // half
    return jnp.where(mine, mine_ref[h % half].astype(F32), other_ref[h % half].astype(F32))


def inside_kernel(factor, h, q_ref, k_ref, v_ref, g_ref, inner_ref, parts_ref, mine_ref, other_ref, qg_ref, kg_ref, vg_ref):
    keep = upper()
    state = state_of(h, mine_ref, other_ref)
    cols = slice(h * HEAD, (h + 1) * HEAD)
    for i in range(q_ref.shape[0] // CHUNK):
        rows = pl.ds(i * CHUNK, CHUNK)
        q, k, v, g = q_ref[rows, cols], k_ref[rows, cols], v_ref[rows, cols], g_ref[rows, cols]
        down = jnp.where(keep, nt(v, g), 0.0).astype(BF16)
        qg = tn(down, k) + nt(g, state.astype(BF16))
        qg_ref[rows, :] = (factor * qg).astype(BF16)
        kg_ref[rows, :] = nn(down, q)
        vg_ref[rows, :] = nn(inner_ref[h, i], g)
        state = state + parts_ref[h, i]


def inside(h, factor, q, k, v, g, inner, parts, states):
    shape = (q.shape[0], HEAD)
    return call(
        functools.partial(inside_kernel, factor, h),
        (q, k, v, g, inner, parts, *states),
        ((shape, BF16), (shape, F32), (shape, F32)),
        flops=q.shape[0] * HEAD * (4 * CHUNK + HEAD) * 2,
    )


def outside_kernel(factor, heads, *refs):
    qg_refs, kg_refs, vg_refs = (refs[i * heads : (i + 1) * heads] for i in range(3))
    k_ref, v_ref, parts_ref, mine_ref, other_ref, query_out, key_out, value_out, key_buf, value_buf, sems = refs[3 * heads :]
    copies = []

    def send(src, dst):
        copies.append(pltpu.make_async_copy(src, dst, sems.at[len(copies)]))
        copies[-1].start()

    for h in range(heads):
        send(qg_refs[h], query_out.at[:, pl.ds(h * HEAD, HEAD)])
    chunks = k_ref.shape[0] // CHUNK
    after = [state_of(h, mine_ref, other_ref) for h in range(heads)]
    for i in reversed(range(chunks)):
        rows = pl.ds(i * CHUNK, CHUNK)
        for h in range(heads):
            cols = slice(h * HEAD, (h + 1) * HEAD)
            state = after[h].astype(BF16)
            key = kg_refs[h][rows, :] + nt(v_ref[rows, cols], state)
            value = vg_refs[h][rows, :] + nn(k_ref[rows, cols], state)
            key_buf[rows, cols] = (factor * key).astype(BF16)
            value_buf[rows, cols] = (factor * value).astype(BF16)
            if i:
                after[h] = after[h] + parts_ref[h, i]
        send(key_buf.at[rows, :], key_out.at[rows, :])
        send(value_buf.at[rows, :], value_out.at[rows, :])
    for copy in copies:
        copy.wait()


def outside(factor, qg, kg, vg, k, v, parts, states):
    heads = len(qg)
    tokens, columns = k.shape
    return call(
        functools.partial(outside_kernel, factor, heads),
        (*qg, *kg, *vg, k, v, parts, *states),
        ((k.shape, BF16),) * 3,
        flops=4 * tokens * columns * HEAD,
        scratch=[
            pltpu.VMEM(k.shape, BF16),
            pltpu.VMEM(k.shape, BF16),
            pltpu.SemaphoreType.DMA((heads + 2 * (tokens // CHUNK),)),
        ],
        out_specs=[pl.BlockSpec(memory_space=pl.ANY)] * 3,
    )


def body(query_rows, key_rows, value_rows, layer_grad, out_weight):
    tokens, columns = query_rows.shape
    heads = columns // HEAD
    factor = float((HEAD * tokens * lax.axis_size(CTX)) ** (-0.5))
    hops = lax.axis_size("tp") // 2

    right = list(split(layer_grad))
    left = list(right)
    parts, offsets, totals = [[part] for part in right], [0], [None, None]
    for hop in range(1, hops):
        right = [moved(right[i], "tp", 1) for i in (0, 1)]
        left = [moved(left[i], "tp", -1) for i in (1, 0)][::-1]
        offsets = offsets + [-hop, hop]
        totals = [product(out_weight, parts[i] + [right[i], left[i]], offsets, totals[i]) for i in (0, 1)]
        parts, offsets = [[], []], []
    last = [moved(right[0], "tp", 1), moved(left[1], "tp", -1)]

    inner, kv_parts, kv_mine, kv_theirs = before(query_rows, key_rows, value_rows, heads, F32)
    kv_states = summed(kv_mine, kv_theirs, False)

    g, g_parts, g_mine, g_theirs = grads(totals, last, out_weight, query_rows, heads, BF16)
    states = summed(g_mine, g_theirs, True)

    near = []
    for h in range(heads):
        near.append(
            inside(h, factor, query_rows, key_rows, value_rows, g, inner, kv_parts, kv_states)
        )
    qg, kg, vg = zip(*near)
    return outside(factor, qg, kg, vg, key_rows, value_rows, g_parts, states)


def solution(mesh):
    finer = Mesh(mesh.devices.reshape(4, 4, 2, mesh.shape["tp"]), (*CTX, "tp"))
    return jax.shard_map(
        body,
        mesh=finer,
        in_specs=(P(CTX, "tp"), P(CTX, "tp"), P(CTX, "tp"), P(CTX, "tp"), P("tp", None)),
        out_specs=(P(CTX, "tp"), P(CTX, "tp"), P(CTX, "tp")),
        check_vma=False,
    )
```
